32 devices in a mesh: reach: 2 (over y), row: 4 (over z), col: 4 (over x, core).
Axes of the slice: x: 2, y: 2, z: 4, core: 2. Of those that a mesh axis runs over, the one named last changes fastest.
Arguments:
- operator: float32 [2048, 65536], P(('reach', 'col'), 'row'), parts along dimension 0, may hold values from -0.03125 to 0.03125
- basis: float32 [131072, 256], P(('reach', 'row')), parts along dimension 0, may hold values from -6 to 6
Outputs:
- image: float32 [2048, 256], P(('reach', 'row')), parts along dimension 0
The draws below stay inside these ranges and needn't reach their ends.
There are 2 independent parts, one for each index of `reach`. The reference program is written for one: setup_inputs(seed, part) draws one part's arguments, and reference() takes and returns one part's arrays. A program takes and returns all parts, laid end to end along the dimension named above; each array names one. Nothing has to cross between parts.
All inputs are finite; a program needn't handle non-finite values.
Results may differ from the reference program's by a relative error of at most 0.000071.
Values sent between devices are 32-bit elements; how exact they have to be, the bound alone decides.
No kernel may reach another device: no remote copies, remote signals or barrier semaphores. Data moves between devices by JAX's collectives and lax.ppermute only.
A program may use at most 64 MiB of HBM per device.

```python
import jax
import jax.numpy as jnp
from jax import lax

NN = 65536
COLS = 256
ROWS = 1024


def strengthened(values, own_key, source, target, blocks, factor):
    owner, partner = [(jnp.arange(values.shape[position]) // (values.shape[position] // blocks)).reshape([-1 if axis == position else 1 for axis in range(values.ndim)]) for position in (source, target)]
    chosen = jax.random.permutation(own_key, blocks)[partner]
    strong = (owner == chosen) | (owner == (partner + blocks // 2) % blocks)
    return jnp.where(strong, factor * values, values)


def level_of(rng, dims, split, low, top_value):
    loudness, own = 1.0, jax.random.fold_in(rng, 6)
    for position, blocks in split:
        heights = jnp.exp(jax.random.uniform(jax.random.fold_in(own, position), (blocks,), jnp.float32, low / len(split), top_value / len(split)))
        loudness = loudness * jnp.repeat(heights, dims[position] // blocks).reshape([-1 if axis == position else 1 for axis in range(len(dims))])
    return loudness


def scatter_about(own_key, shape, width, most, cuts=(), dtype=jnp.bfloat16):
    array = jax.random.normal(own_key, shape, jnp.float32) * width
    if len(cuts) > 0:
        array = level_of(own_key, shape, cuts, -0.22, 0.18) * array
    return jnp.clip(array, min=-most, max=most).astype(dtype)


def gaussian_with(key, extent, scale, reach, shards, heavy, dtype=jnp.bfloat16):
    array = scale * jax.random.normal(key, extent, jnp.float32)
    if shards:
        array = array * level_of(key, extent, shards, -0.22, 0.18)
    return jnp.clip(strengthened(array, jax.random.fold_in(key, 3), *heavy), -reach, reach).astype(dtype)


def setup_inputs(seed: int = 0, part: int = 0) -> dict:
    key_list = jax.random.split(jax.random.key(seed), 3)
    part_splits = jax.random.split(jax.random.fold_in(key_list[2], part), 3)
    operator = gaussian_with(part_splits[0], (ROWS, NN), NN ** -0.5, 0.03125, ((0, 4), (1, 4)), (1, 0, 4, 2.0), jnp.float32)
    basis = scatter_about(part_splits[1], (NN, COLS), 1.0, 6.0, ((0, 4),), jnp.float32)
    return {"operator": operator, "basis": basis}


def reference(operator, basis):
    return jnp.dot(operator, basis, preferred_element_type=jnp.float32, precision=lax.Precision.HIGHEST)
```

```python
import functools

import jax
import jax.numpy as jnp
from jax import lax
from jax.experimental import pallas as pl
from jax.experimental.pallas import tpu as pltpu
from jax.sharding import PartitionSpec as P

CHUNK = 1024
DEPTH = 6


def split(value):
    high = value.astype(jnp.bfloat16)
    low = (value - high.astype(jnp.float32)).astype(jnp.bfloat16)
    return high, low


def dot(a, b):
    return jnp.dot(a, b, preferred_element_type=jnp.float32)


def matmul_kernel(steps, chunk, a_hbm, b_hbm, out, a_buf, b_buf, sems):
    def copies(step):
        where = pl.ds(step * chunk, chunk)
        return (
            pltpu.make_async_copy(a_hbm.at[:, where], a_buf.at[step], sems.at[0, step]),
            pltpu.make_async_copy(b_hbm.at[where, :], b_buf.at[step], sems.at[1, step]),
        )

    def start(step):
        for copy in copies(step):
            copy.start()

    for step in range(min(DEPTH, steps)):
        start(step)
    rows = out.shape[0]
    half = rows // 2 if rows % 16 == 0 else rows
    total = jnp.zeros(out.shape, jnp.float32)
    for step in range(steps):
        for copy in copies(step):
            copy.wait()
        if step + DEPTH < steps:
            start(step + DEPTH)
        b_high, b_low = split(b_buf[step])
        parts = []
        for first in range(0, rows, half):
            a_high, a_low = split(a_buf[step, first : first + half])
            parts.append(dot(a_high, b_high) + dot(a_high, b_low) + dot(a_low, b_high))
        total += jnp.concatenate(parts, 0)
    out[...] = total


def matmul(a, b):
    rows, depth = a.shape
    columns = b.shape[1]
    chunk = min(CHUNK, depth)
    steps = depth // chunk
    return pl.pallas_call(
        functools.partial(matmul_kernel, steps, chunk),
        out_shape=jax.ShapeDtypeStruct((rows, columns), jnp.float32),
        in_specs=[pl.BlockSpec(memory_space=pl.ANY)] * 2,
        out_specs=pl.BlockSpec(memory_space=pltpu.VMEM),
        scratch_shapes=[
            pltpu.VMEM((steps, rows, chunk), jnp.float32),
            pltpu.VMEM((steps, chunk, columns), jnp.float32),
            pltpu.SemaphoreType.DMA((2, steps)),
        ],
        compiler_params=pltpu.CompilerParams(vmem_limit_bytes=60 * 2**20),
    )(a, b)


def permute(value, n_row, n_col, target):
    pairs = []
    for r in range(n_row):
        for c in range(n_col):
            to_r, to_c = target(r, c)
            pairs.append((r * n_col + c, to_r * n_col + to_c))
    return lax.ppermute(value, ("row", "col"), pairs)


def general(partial, n_row, n_col):
    rows = partial.shape[0]
    group = n_row // n_col
    out_rows = rows // group
    summed = lax.psum(partial, "row")
    row = lax.axis_index("row")
    picked = lax.dynamic_slice_in_dim(summed, row % group * out_rows, out_rows, 0)
    kept = jnp.where(lax.axis_index("col") == row // group, picked, 0)
    return lax.psum(kept, "col")


def square(partial, n_row, n_col):
    row, col = lax.axis_index("row"), lax.axis_index("col")
    half = partial.shape[0] // 2
    side = row // 2
    near = lax.dynamic_slice_in_dim(partial, side * half, half, 0)
    far = lax.dynamic_slice_in_dim(partial, (1 - side) * half, half, 0)
    near = permute(near, n_row, n_col, lambda r, c: (c, (r // 2) * 2 + r % 2))
    far = permute(far, n_row, n_col, lambda r, c: (c, (1 - r // 2) * 2 + r % 2))
    mine = near + far
    mine = mine + lax.ppermute(mine, "col", [(c, c ^ 1) for c in range(n_col)])
    other = lax.ppermute(mine, "col", [(c, c ^ 2) for c in range(n_col)])
    first = col < 2
    return jnp.concatenate([jnp.where(first, mine, other), jnp.where(first, other, mine)], 0)


def shards(operator, basis):
    partial = matmul(operator, basis)
    n_row, n_col = lax.axis_size("row"), lax.axis_size("col")
    if n_row == 4 and n_col == 4 and partial.shape[0] % 16 == 0:
        return square(partial, n_row, n_col)
    return general(partial, n_row, n_col)


def solution(mesh):
    in_specs = (P(("reach", "col"), "row"), P(("reach", "row"), None))
    out_specs = P(("reach", "row"), None)
    return jax.shard_map(shards, mesh=mesh, in_specs=in_specs, out_specs=out_specs, check_vma=False)
```

```python
import functools

import jax
import jax.numpy as jnp
from jax import lax
from jax.experimental import pallas as pl
from jax.experimental.pallas import tpu as pltpu
from jax.sharding import PartitionSpec as P

CHUNK = 1024
DEPTH = 6


def split(value):
    high = value.astype(jnp.bfloat16)
    low = (value - high.astype(jnp.float32)).astype(jnp.bfloat16)
    return high, low


def dot(a, b):
    return jnp.dot(a, b, preferred_element_type=jnp.float32)


def pieces(depth):
    sizes = []
    left = depth
    while left > CHUNK:
        sizes.append(CHUNK)
        left -= CHUNK
    while left > 256 and left % 256 == 0:
        sizes.append(left // 2)
        left -= left // 2
    sizes.append(left)
    spans, start = [], 0
    for size in sizes:
        spans.append((start, size))
        start += size
    return spans


def matmul_kernel(spans, pick, a_hbm, b_hbm, first, second, a_buf, b_buf, sems):
    def copies(step):
        where = pl.ds(*spans[step])
        return (
            pltpu.make_async_copy(a_hbm.at[:, where], a_buf.at[:, where], sems.at[0, step]),
            pltpu.make_async_copy(b_hbm.at[where, :], b_buf.at[where, :], sems.at[1, step]),
        )

    def start(step):
        for copy in copies(step):
            copy.start()

    steps = len(spans)
    for step in range(min(DEPTH, steps)):
        start(step)
    half = a_hbm.shape[0] // 2
    totals = [jnp.zeros(first.shape, jnp.float32) for _ in range(2)]
    for step, (begin, size) in enumerate(spans):
        for copy in copies(step):
            copy.wait()
        if step + DEPTH < steps:
            start(step + DEPTH)
        b_high, b_low = split(b_buf[begin : begin + size])
        for side in range(2):
            a_high, a_low = split(a_buf[side * half : (side + 1) * half, begin : begin + size])
            totals[side] += dot(a_high, b_high) + dot(a_high, b_low) + dot(a_low, b_high)
    chosen = pick()

    @pl.when(chosen == 0)
    def _():
        first[...] = totals[0]
        second[...] = totals[1]

    @pl.when(chosen != 0)
    def _():
        first[...] = totals[1]
        second[...] = totals[0]


def matmul(a, b, pick):
    rows, depth = a.shape
    columns = b.shape[1]
    spans = pieces(depth)
    half = pltpu.VMEM((rows // 2, columns), jnp.float32)
    return pl.pallas_call(
        functools.partial(matmul_kernel, spans, pick),
        out_shape=(half, half),
        in_specs=[pl.BlockSpec(memory_space=pl.ANY)] * 2,
        out_specs=(pl.BlockSpec(memory_space=pltpu.VMEM),) * 2,
        scratch_shapes=[
            pltpu.VMEM((rows, depth), jnp.float32),
            pltpu.VMEM((depth, columns), jnp.float32),
            pltpu.SemaphoreType.DMA((2, len(spans))),
        ],
        compiler_params=pltpu.CompilerParams(vmem_limit_bytes=48 * 2**20),
    )(a, b)


def permute(value, n_row, n_col, target):
    pairs = []
    for r in range(n_row):
        for c in range(n_col):
            to_r, to_c = target(r, c)
            pairs.append((r * n_col + c, to_r * n_col + to_c))
    return lax.ppermute(value, ("row", "col"), pairs)


def general(operator, basis, n_row, n_col):
    partial = jnp.concatenate(matmul(operator, basis, lambda: 0), 0)
    group = n_row // n_col
    out_rows = partial.shape[0] // group
    summed = lax.psum(partial, "row")
    row = lax.axis_index("row")
    picked = lax.dynamic_slice_in_dim(summed, row % group * out_rows, out_rows, 0)
    kept = jnp.where(lax.axis_index("col") == row // group, picked, 0)
    return lax.psum(kept, "col")


def square(operator, basis, n_row, n_col):
    def side(r, c):
        return (r // 2) ^ (c // 2)

    def core_first(r, c):
        return (r ^ 1) % 2

    def core_second(r, c):
        return (r ^ 1) % 2

    def pick():
        return side(lax.axis_index("row"), lax.axis_index("col"))

    one, two = matmul(operator, basis, pick)
    one = permute(one, n_row, n_col, lambda r, c: (c, 2 * side(r, c) + core_first(r, c)))
    two = permute(two, n_row, n_col, lambda r, c: (c, 2 * (1 - side(r, c)) + core_second(r, c)))
    mine = two + one
    mine = mine + lax.ppermute(mine, "col", [(c, c ^ 1) for c in range(n_col)])
    other = lax.ppermute(mine, "col", [(c, c ^ 2) for c in range(n_col)])
    left = lax.axis_index("col") < 2
    return jnp.concatenate([jnp.where(left, mine, other), jnp.where(left, other, mine)], 0)


def shards(operator, basis):
    n_row, n_col = lax.axis_size("row"), lax.axis_size("col")
    if n_row == 4 and n_col == 4:
        return square(operator, basis, n_row, n_col)
    return general(operator, basis, n_row, n_col)


def solution(mesh):
    in_specs = (P(("reach", "col"), "row"), P(("reach", "row"), None))
    out_specs = P(("reach", "row"), None)
    return jax.shard_map(shards, mesh=mesh, in_specs=in_specs, out_specs=out_specs, check_vma=False)
```

```python
import functools

import jax
import jax.numpy as jnp
from jax import lax
from jax.experimental import pallas as pl
from jax.experimental.pallas import tpu as pltpu
from jax.sharding import PartitionSpec as P

CHUNK = 1024
DEPTH = 6


def split(value):
    high = value.astype(jnp.bfloat16)
    low = (value - high.astype(jnp.float32)).astype(jnp.bfloat16)
    return high, low


def dot(a, b):
    return jnp.dot(a, b, preferred_element_type=jnp.float32)


def pieces(depth):
    sizes = []
    left = depth
    while left > CHUNK:
        sizes.append(CHUNK)
        left -= CHUNK
    while left > 256 and left % 256 == 0:
        sizes.append(left // 2)
        left -= left // 2
    sizes.append(left)
    spans, start = [], 0
    for size in sizes:
        spans.append((start, size))
        start += size
    return spans


def matmul_kernel(spans, pick, a_hbm, b_hbm, first, second, third, a_buf, b_buf, sems):
    def copies(step):
        where = pl.ds(*spans[step])
        return (
            pltpu.make_async_copy(a_hbm.at[:, where], a_buf.at[:, where], sems.at[0, step]),
            pltpu.make_async_copy(b_hbm.at[where, :], b_buf.at[where, :], sems.at[1, step]),
        )

    def start(step):
        for copy in copies(step):
            copy.start()

    steps = len(spans)
    for step in range(min(DEPTH, steps)):
        start(step)
    half = a_hbm.shape[0] // 2
    totals = [jnp.zeros(first.shape, jnp.float32) for _ in range(2)]
    for step, (begin, size) in enumerate(spans):
        for copy in copies(step):
            copy.wait()
        if step + DEPTH < steps:
            start(step + DEPTH)
        b_high, b_low = split(b_buf[begin : begin + size])
        for side in range(2):
            a_high, a_low = split(a_buf[side * half : (side + 1) * half, begin : begin + size])
            totals[side] += dot(a_high, b_high) + dot(a_high, b_low) + dot(a_low, b_high)
    chosen = pick()

    def put(whole, cut):
        first[...] = whole
        second[...] = cut[: second.shape[0]]
        third[...] = cut[second.shape[0] :]

    @pl.when(chosen == 0)
    def _():
        put(totals[0], totals[1])

    @pl.when(chosen != 0)
    def _():
        put(totals[1], totals[0])


def matmul(a, b, pick):
    rows, depth = a.shape
    columns = b.shape[1]
    spans = pieces(depth)
    half = pltpu.VMEM((rows // 2, columns), jnp.float32)
    relayed = rows // 2 // 2
    direct = pltpu.VMEM((rows // 2 - relayed, columns), jnp.float32)
    relay = pltpu.VMEM((relayed, columns), jnp.float32)
    return pl.pallas_call(
        functools.partial(matmul_kernel, spans, pick),
        out_shape=(half, direct, relay),
        in_specs=[pl.BlockSpec(memory_space=pl.ANY)] * 2,
        out_specs=(pl.BlockSpec(memory_space=pltpu.VMEM),) * 3,
        scratch_shapes=[
            pltpu.VMEM((rows, depth), jnp.float32),
            pltpu.VMEM((depth, columns), jnp.float32),
            pltpu.SemaphoreType.DMA((2, len(spans))),
        ],
        compiler_params=pltpu.CompilerParams(vmem_limit_bytes=48 * 2**20),
    )(a, b)


def permute(value, n_row, n_col, target):
    pairs = []
    for r in range(n_row):
        for c in range(n_col):
            to_r, to_c = target(r, c)
            pairs.append((r * n_col + c, to_r * n_col + to_c))
    return lax.ppermute(value, ("row", "col"), pairs)


def general(operator, basis, n_row, n_col):
    partial = jnp.concatenate(matmul(operator, basis, lambda: 0), 0)
    group = n_row // n_col
    out_rows = partial.shape[0] // group
    summed = lax.psum(partial, "row")
    row = lax.axis_index("row")
    picked = lax.dynamic_slice_in_dim(summed, row % group * out_rows, out_rows, 0)
    kept = jnp.where(lax.axis_index("col") == row // group, picked, 0)
    return lax.psum(kept, "col")


def square(operator, basis, n_row, n_col):
    def core_first(r, c):
        return (r ^ 1) % 2

    def core_second(r, c):
        return (r ^ 1) % 2

    def pick():
        return 1 - lax.axis_index("row") // 2

    first, direct, relay = matmul(operator, basis, pick)
    relay = lax.ppermute(relay, "col", [(c, c ^ 2) for c in range(n_col)])
    first = permute(first, n_row, n_col, lambda r, c: (c, 2 * (1 - r // 2) + core_first(r, c)))
    direct = permute(direct, n_row, n_col, lambda r, c: (c, 2 * (r // 2) + core_second(r, c)))
    relay = permute(relay, n_row, n_col, lambda r, c: (c ^ 2, 2 * (r // 2) + core_second(r, c ^ 2)))
    mine = first + jnp.concatenate([direct, relay], 0)
    mine = mine + lax.ppermute(mine, "col", [(c, c ^ 1) for c in range(n_col)])
    other = lax.ppermute(mine, "col", [(c, c ^ 2) for c in range(n_col)])
    left = lax.axis_index("col") < 2
    return jnp.concatenate([jnp.where(left, mine, other), jnp.where(left, other, mine)], 0)


def shards(operator, basis):
    n_row, n_col = lax.axis_size("row"), lax.axis_size("col")
    if n_row == 4 and n_col == 4:
        return square(operator, basis, n_row, n_col)
    return general(operator, basis, n_row, n_col)


def solution(mesh):
    in_specs = (P(("reach", "col"), "row"), P(("reach", "row"), None))
    out_specs = P(("reach", "row"), None)
    return jax.shard_map(shards, mesh=mesh, in_specs=in_specs, out_specs=out_specs, check_vma=False)
```

```python
import functools

import jax
import jax.numpy as jnp
from jax import lax
from jax.experimental import pallas as pl
from jax.experimental.pallas import tpu as pltpu
from jax.sharding import PartitionSpec as P

CHUNK = 1024
DEPTH = 6


def split(value):
    high = value.astype(jnp.bfloat16)
    low = (value - high.astype(jnp.float32)).astype(jnp.bfloat16)
    return high, low


def dot(a, b):
    return jnp.dot(a, b, preferred_element_type=jnp.float32)


def pieces(depth):
    sizes = []
    left = depth
    while left > CHUNK:
        sizes.append(CHUNK)
        left -= CHUNK
    while left > 256 and left % 256 == 0:
        sizes.append(left // 2)
        left -= left // 2
    sizes.append(left)
    spans, start = [], 0
    for size in sizes:
        spans.append((start, size))
        start += size
    return spans


def matmul_kernel(spans, pick, a_hbm, b_hbm, early, late, second, third, a_buf, b_buf, sems):
    def copies(step):
        where = pl.ds(*spans[step])
        return (
            pltpu.make_async_copy(a_hbm.at[:, where], a_buf.at[:, where], sems.at[0, step]),
            pltpu.make_async_copy(b_hbm.at[where, :], b_buf.at[where, :], sems.at[1, step]),
        )

    def start(step):
        for copy in copies(step):
            copy.start()

    steps = len(spans)
    for step in range(min(DEPTH, steps)):
        start(step)
    half = a_hbm.shape[0] // 2
    totals = [jnp.zeros((half, early.shape[1]), jnp.float32) for _ in range(2)]
    for step, (begin, size) in enumerate(spans):
        for copy in copies(step):
            copy.wait()
        if step + DEPTH < steps:
            start(step + DEPTH)
        b_high, b_low = split(b_buf[begin : begin + size])
        for side in range(2):
            a_high, a_low = split(a_buf[side * half : (side + 1) * half, begin : begin + size])
            totals[side] += dot(a_high, b_high) + dot(a_high, b_low) + dot(a_low, b_high)
    chosen = pick()

    def put(whole, cut):
        early[...] = whole[: early.shape[0]]
        late[...] = whole[early.shape[0] :]
        second[...] = cut[: second.shape[0]]
        third[...] = cut[second.shape[0] :]

    @pl.when(chosen == 0)
    def _():
        put(totals[0], totals[1])

    @pl.when(chosen != 0)
    def _():
        put(totals[1], totals[0])


def matmul(a, b, pick):
    rows, depth = a.shape
    columns = b.shape[1]
    spans = pieces(depth)
    quarter = pltpu.VMEM((rows // 4, columns), jnp.float32)
    return pl.pallas_call(
        functools.partial(matmul_kernel, spans, pick),
        out_shape=(quarter,) * 4,
        in_specs=[pl.BlockSpec(memory_space=pl.ANY)] * 2,
        out_specs=(pl.BlockSpec(memory_space=pltpu.VMEM),) * 4,
        scratch_shapes=[
            pltpu.VMEM((rows, depth), jnp.float32),
            pltpu.VMEM((depth, columns), jnp.float32),
            pltpu.SemaphoreType.DMA((2, len(spans))),
        ],
        compiler_params=pltpu.CompilerParams(vmem_limit_bytes=48 * 2**20),
    )(a, b)


def permute(value, n_row, n_col, target):
    pairs = []
    for r in range(n_row):
        for c in range(n_col):
            to_r, to_c = target(r, c)
            pairs.append((r * n_col + c, to_r * n_col + to_c))
    return lax.ppermute(value, ("row", "col"), pairs)


def general(operator, basis, n_row, n_col):
    partial = jnp.concatenate(matmul(operator, basis, lambda: 0), 0)
    group = n_row // n_col
    out_rows = partial.shape[0] // group
    summed = lax.psum(partial, "row")
    row = lax.axis_index("row")
    picked = lax.dynamic_slice_in_dim(summed, row % group * out_rows, out_rows, 0)
    kept = jnp.where(lax.axis_index("col") == row // group, picked, 0)
    return lax.psum(kept, "col")


def square(operator, basis, n_row, n_col):
    def core_first(r, c):
        return (r ^ 1) % 2

    def core_second(r, c):
        return (r ^ 1) % 2

    def pick():
        return 1 - lax.axis_index("row") // 2

    early, late, direct, relay = matmul(operator, basis, pick)

    def near(value):
        return permute(value, n_row, n_col, lambda r, c: (c, 2 * (1 - r // 2) + core_first(r, c)))

    relay = lax.ppermute(relay, "col", [(c, c ^ 2) for c in range(n_col)])
    relay, late = lax.optimization_barrier((relay, late))
    early = near(early)
    direct = permute(direct, n_row, n_col, lambda r, c: (c, 2 * (r // 2) + core_second(r, c)))
    relay = permute(relay, n_row, n_col, lambda r, c: (c ^ 2, 2 * (r // 2) + core_second(r, c ^ 2)))
    late = near(late)
    mine, other = [], []
    for part in (direct + early, relay + late):
        part = part + lax.ppermute(part, "col", [(c, c ^ 1) for c in range(n_col)])
        mine.append(part)
        other.append(lax.ppermute(part, "col", [(c, c ^ 2) for c in range(n_col)]))
    left = lax.axis_index("col") < 2
    top = [jnp.where(left, m, o) for m, o in zip(mine, other)]
    bottom = [jnp.where(left, o, m) for m, o in zip(mine, other)]
    return jnp.concatenate(top + bottom, 0)


def shards(operator, basis):
    n_row, n_col = lax.axis_size("row"), lax.axis_size("col")
    if n_row == 4 and n_col == 4:
        return square(operator, basis, n_row, n_col)
    return general(operator, basis, n_row, n_col)


def solution(mesh):
    in_specs = (P(("reach", "col"), "row"), P(("reach", "row"), None))
    out_specs = P(("reach", "row"), None)
    return jax.shard_map(shards, mesh=mesh, in_specs=in_specs, out_specs=out_specs, check_vma=False)
```

```python
import functools

import jax
import jax.numpy as jnp
from jax import lax
from jax.experimental import pallas as pl
from jax.experimental.pallas import tpu as pltpu
from jax.sharding import PartitionSpec as P

CHUNK = 1024
DEPTH = 20


def split(value):
    high = value.astype(jnp.bfloat16)
    low = (value - high.astype(jnp.float32)).astype(jnp.bfloat16)
    return high, low


def dot(a, b):
    return jnp.dot(a, b, preferred_element_type=jnp.float32)


def pieces(depth):
    sizes = []
    left = depth
    while left > CHUNK:
        sizes.append(CHUNK)
        left -= CHUNK
    while left > 256 and left % 256 == 0:
        sizes.append(left // 2)
        left -= left // 2
    sizes.append(left)
    spans, start = [], 0
    for size in sizes:
        spans.append((start, size))
        start += size
    return spans


def matmul_kernel(spans, pick, a_hbm, b_hbm, early, late, second, third, a_buf, b_buf, sems):
    def copies(step):
        where = pl.ds(*spans[step])
        return (
            pltpu.make_async_copy(a_hbm.at[:, where], a_buf.at[:, where], sems.at[0, step]),
            pltpu.make_async_copy(b_hbm.at[where, :], b_buf.at[where, :], sems.at[1, step]),
        )

    def start(step):
        for copy in copies(step):
            copy.start()

    steps = len(spans)
    for step in range(min(DEPTH, steps)):
        start(step)
    half = a_hbm.shape[0] // 2
    totals = [jnp.zeros((half, early.shape[1]), jnp.float32) for _ in range(2)]
    for step, (begin, size) in enumerate(spans):
        for copy in copies(step):
            copy.wait()
        if step + DEPTH < steps:
            start(step + DEPTH)
        b_high, b_low = split(b_buf[begin : begin + size])
        for side in range(2):
            a_high, a_low = split(a_buf[side * half : (side + 1) * half, begin : begin + size])
            totals[side] += dot(a_high, b_high) + dot(a_high, b_low) + dot(a_low, b_high)
    chosen = pick()

    def put(whole, cut):
        early[...] = whole[: early.shape[0]]
        late[...] = whole[early.shape[0] :]
        second[...] = cut[: second.shape[0]]
        third[...] = cut[second.shape[0] :]

    @pl.when(chosen == 0)
    def _():
        put(totals[0], totals[1])

    @pl.when(chosen != 0)
    def _():
        put(totals[1], totals[0])


def matmul(a, b, pick):
    rows, depth = a.shape
    columns = b.shape[1]
    spans = pieces(depth)
    quarter = pltpu.VMEM((rows // 4, columns), jnp.float32)
    return pl.pallas_call(
        functools.partial(matmul_kernel, spans, pick),
        out_shape=(quarter,) * 4,
        in_specs=[pl.BlockSpec(memory_space=pl.ANY)] * 2,
        out_specs=(pl.BlockSpec(memory_space=pltpu.VMEM),) * 4,
        scratch_shapes=[
            pltpu.VMEM((rows, depth), jnp.float32),
            pltpu.VMEM((depth, columns), jnp.float32),
            pltpu.SemaphoreType.DMA((2, len(spans))),
        ],
        compiler_params=pltpu.CompilerParams(vmem_limit_bytes=48 * 2**20),
    )(a, b)


def permute(value, n_row, n_col, target):
    pairs = []
    for r in range(n_row):
        for c in range(n_col):
            to_r, to_c = target(r, c)
            pairs.append((r * n_col + c, to_r * n_col + to_c))
    return lax.ppermute(value, ("row", "col"), pairs)


def general(operator, basis, n_row, n_col):
    partial = jnp.concatenate(matmul(operator, basis, lambda: 0), 0)
    group = n_row // n_col
    out_rows = partial.shape[0] // group
    summed = lax.psum(partial, "row")
    row = lax.axis_index("row")
    picked = lax.dynamic_slice_in_dim(summed, row % group * out_rows, out_rows, 0)
    kept = jnp.where(lax.axis_index("col") == row // group, picked, 0)
    return lax.psum(kept, "col")


def square(operator, basis, n_row, n_col):
    def core_first(r, c):
        return (r ^ 1) % 2

    def core_second(r, c):
        return (r ^ 1) % 2

    def pick():
        return 1 - lax.axis_index("row") // 2

    early, late, direct, relay = matmul(operator, basis, pick)

    def near(value):
        return permute(value, n_row, n_col, lambda r, c: (c, 2 * (1 - r // 2) + core_first(r, c)))

    relay = lax.ppermute(relay, "col", [(c, c ^ 2) for c in range(n_col)])
    relay, late = lax.optimization_barrier((relay, late))
    early = near(early)
    direct = permute(direct, n_row, n_col, lambda r, c: (c, 2 * (r // 2) + core_second(r, c)))
    relay = permute(relay, n_row, n_col, lambda r, c: (c ^ 2, 2 * (r // 2) + core_second(r, c ^ 2)))
    late = near(late)
    mine, other = [], []
    for part in (direct + early, relay + late):
        part = part + lax.ppermute(part, "col", [(c, c ^ 1) for c in range(n_col)])
        mine.append(part)
        other.append(lax.ppermute(part, "col", [(c, c ^ 2) for c in range(n_col)]))
    left = lax.axis_index("col") < 2
    top = [jnp.where(left, m, o) for m, o in zip(mine, other)]
    bottom = [jnp.where(left, o, m) for m, o in zip(mine, other)]
    return jnp.concatenate(top + bottom, 0)


def shards(operator, basis):
    n_row, n_col = lax.axis_size("row"), lax.axis_size("col")
    if n_row == 4 and n_col == 4:
        return square(operator, basis, n_row, n_col)
    return general(operator, basis, n_row, n_col)


def solution(mesh):
    in_specs = (P(("reach", "col"), "row"), P(("reach", "row"), None))
    out_specs = P(("reach", "row"), None)
    return jax.shard_map(shards, mesh=mesh, in_specs=in_specs, out_specs=out_specs, check_vma=False)
```

```python
import functools

import jax
import jax.numpy as jnp
from jax import lax
from jax.experimental import pallas as pl
from jax.experimental.pallas import tpu as pltpu
from jax.sharding import PartitionSpec as P

CHUNK = 1024
DEPTH = 20


def split(value):
    high = value.astype(jnp.bfloat16)
    low = (value - high.astype(jnp.float32)).astype(jnp.bfloat16)
    return high, low


def dot(a, b):
    return jnp.dot(a, b, preferred_element_type=jnp.float32)


def pieces(depth):
    sizes = []
    left = depth
    while left > CHUNK:
        sizes.append(CHUNK)
        left -= CHUNK
    while left > 128 and left % 256 == 0:
        sizes.append(left // 2)
        left -= left // 2
    sizes.append(left)
    spans, start = [], 0
    for size in sizes:
        spans.append((start, size))
        start += size
    return spans


def matmul_kernel(spans, pick, a_hbm, b_hbm, early, late, second, third, a_buf, b_buf, sems):
    def copies(step):
        where = pl.ds(*spans[step])
        return (
            pltpu.make_async_copy(a_hbm.at[:, where], a_buf.at[:, where], sems.at[0, step]),
            pltpu.make_async_copy(b_hbm.at[where, :], b_buf.at[where, :], sems.at[1, step]),
        )

    def start(step):
        for copy in copies(step):
            copy.start()

    steps = len(spans)
    for step in range(min(DEPTH, steps)):
        start(step)
    half = a_hbm.shape[0] // 2
    totals = [jnp.zeros((half, early.shape[1]), jnp.float32) for _ in range(2)]
    for step, (begin, size) in enumerate(spans):
        for copy in copies(step):
            copy.wait()
        if step + DEPTH < steps:
            start(step + DEPTH)
        b_high, b_low = split(b_buf[begin : begin + size])
        for side in range(2):
            a_high, a_low = split(a_buf[side * half : (side + 1) * half, begin : begin + size])
            totals[side] += dot(a_high, b_high) + dot(a_high, b_low) + dot(a_low, b_high)
    chosen = pick()

    def put(whole, cut):
        early[...] = whole[: early.shape[0]]
        late[...] = whole[early.shape[0] :]
        second[...] = cut[: second.shape[0]]
        third[...] = cut[second.shape[0] :]

    @pl.when(chosen == 0)
    def _():
        put(totals[0], totals[1])

    @pl.when(chosen != 0)
    def _():
        put(totals[1], totals[0])


def matmul(a, b, pick):
    rows, depth = a.shape
    columns = b.shape[1]
    spans = pieces(depth)
    quarter = pltpu.VMEM((rows // 4, columns), jnp.float32)
    return pl.pallas_call(
        functools.partial(matmul_kernel, spans, pick),
        out_shape=(quarter,) * 4,
        in_specs=[pl.BlockSpec(memory_space=pl.ANY)] * 2,
        out_specs=(pl.BlockSpec(memory_space=pltpu.VMEM),) * 4,
        scratch_shapes=[
            pltpu.VMEM((rows, depth), jnp.float32),
            pltpu.VMEM((depth, columns), jnp.float32),
            pltpu.SemaphoreType.DMA((2, len(spans))),
        ],
        compiler_params=pltpu.CompilerParams(vmem_limit_bytes=48 * 2**20),
    )(a, b)


def permute(value, n_row, n_col, target):
    pairs = []
    for r in range(n_row):
        for c in range(n_col):
            to_r, to_c = target(r, c)
            pairs.append((r * n_col + c, to_r * n_col + to_c))
    return lax.ppermute(value, ("row", "col"), pairs)


def general(operator, basis, n_row, n_col):
    partial = jnp.concatenate(matmul(operator, basis, lambda: 0), 0)
    group = n_row // n_col
    out_rows = partial.shape[0] // group
    summed = lax.psum(partial, "row")
    row = lax.axis_index("row")
    picked = lax.dynamic_slice_in_dim(summed, row % group * out_rows, out_rows, 0)
    kept = jnp.where(lax.axis_index("col") == row // group, picked, 0)
    return lax.psum(kept, "col")


def square(operator, basis, n_row, n_col):
    def core_first(r, c):
        return (r ^ 1) % 2

    def core_second(r, c):
        return (r ^ 1) % 2

    def pick():
        return 1 - lax.axis_index("row") // 2

    early, late, direct, relay = matmul(operator, basis, pick)

    def near(value):
        return permute(value, n_row, n_col, lambda r, c: (c, 2 * (1 - r // 2) + core_first(r, c)))

    relay = lax.ppermute(relay, "col", [(c, c ^ 2) for c in range(n_col)])
    relay, late = lax.optimization_barrier((relay, late))
    early = near(early)
    direct = permute(direct, n_row, n_col, lambda r, c: (c, 2 * (r // 2) + core_second(r, c)))
    relay = permute(relay, n_row, n_col, lambda r, c: (c ^ 2, 2 * (r // 2) + core_second(r, c ^ 2)))
    late = near(late)
    mine, other = [], []
    for part in (direct + early, relay + late):
        part = part + lax.ppermute(part, "col", [(c, c ^ 1) for c in range(n_col)])
        mine.append(part)
        other.append(lax.ppermute(part, "col", [(c, c ^ 2) for c in range(n_col)]))
    left = lax.axis_index("col") < 2
    top = [jnp.where(left, m, o) for m, o in zip(mine, other)]
    bottom = [jnp.where(left, o, m) for m, o in zip(mine, other)]
    return jnp.concatenate(top + bottom, 0)


def shards(operator, basis):
    n_row, n_col = lax.axis_size("row"), lax.axis_size("col")
    if n_row == 4 and n_col == 4:
        return square(operator, basis, n_row, n_col)
    return general(operator, basis, n_row, n_col)


def solution(mesh):
    in_specs = (P(("reach", "col"), "row"), P(("reach", "row"), None))
    out_specs = P(("reach", "row"), None)
    return jax.shard_map(shards, mesh=mesh, in_specs=in_specs, out_specs=out_specs, check_vma=False)
```
